32 devices in a mesh: sec: 8 (over z, x), tile: 4 (over y, core).
Axes of the slice: x: 2, y: 2, z: 4, core: 2. Of those that a mesh axis runs over, the one named last changes fastest.
Arguments:
- features: bfloat16 [8, 2048, 256], P('sec', 'tile'), may hold values from -16 to 16
- select: int32 [8, 2048], P('sec', 'tile'), may hold values from 1 to 7
- validity: int32 [8], P('sec'), may hold values 0 or 1
- offset_gain: float32 [3, 256], replicated, may hold values from 0.5 to 2
Outputs:
- aligned: bfloat16 [8, 2048, 256], P('sec', 'tile')
The draws below stay inside these ranges and needn't reach their ends.
Inputs may be any that keep to these rules, and one draw needn't show every extreme that they name: `select`: bit k - 1 of a value is 1 where offset k votes.
All inputs are finite; a program needn't handle non-finite values. No bound on the sum of `validity` on one device may be relied on, other than what follows from the above.
Results may differ from the reference program's by a relative error of at most 0.0027.
Values may be sent and summed in bfloat16 or wider, within the bound.
No kernel may reach another device: no remote copies, remote signals or barrier semaphores. Data moves between devices by JAX's collectives and lax.ppermute only.
A program may use at most 64 MiB of HBM per device.

```python
import math
import jax
import jax.numpy as jnp
from jax import lax

CHANNELS = 256
POSITIONS = 2048
SECTIONS = 8


def draw_features(key, part):
    values_all = jax.random.normal(key, (SECTIONS, POSITIONS, CHANNELS), jnp.float32)
    return jnp.clip(values_all, -16.0, 16.0).astype(jnp.bfloat16)


def touch_ends(values, stream_key, low, top_value):
    longest = values.shape.index(max(values.shape))
    spots = []
    for shift in (0, 1):
        where = [jax.random.randint(jax.random.fold_in(stream_key, axis), (), 0, length) for axis, length in enumerate(values.shape)]
        where[longest] = (where[longest] + shift) % values.shape[longest]
        spots.append(tuple(where))
    return values.at[spots[0]].set(low).at[spots[1]].set(top_value)


def setup_inputs(seed: int = 0) -> dict:
    keys = jax.random.split(jax.random.key(seed), 5)
    return {
        "features": draw_features(jax.random.fold_in(keys[4], 71), 0),
        "select": touch_ends(jax.random.randint(keys[1], (SECTIONS, POSITIONS), 1, 8), jax.random.fold_in(keys[1], 1), 1, 7).astype(jnp.int32),
        "validity": touch_ends((jax.random.randint(keys[2], (SECTIONS,), 0, 4) < 3).astype(jnp.int32), jax.random.fold_in(keys[2], 1), 0, 1),
        "offset_gain": jnp.clip(jnp.exp(jax.random.uniform(keys[3], (3, CHANNELS), jnp.float32, math.log(0.5), math.log(2.0))), 0.5, 2.0),
    }


score_factor = 2.5

def match_section(queries, key_rows):
    score_scale = score_factor / math.sqrt(key_rows.shape[-1])
    scores = jnp.dot(queries, key_rows.T, preferred_element_type=jnp.float32) * score_scale
    row_max = lax.optimization_barrier(jnp.max(scores, axis=1))
    weights = jnp.exp(scores - row_max[:, None])
    row_sum = lax.optimization_barrier(jnp.sum(weights, axis=1))
    weighted = jnp.dot(weights.astype(jnp.bfloat16), key_rows, preferred_element_type=jnp.float32)
    return weighted / row_sum[:, None]

def reference(features, select, validity, offset_gain):

    def per_section(section_id):
        queries = lax.dynamic_index_in_dim(features, section_id, 0, keepdims=False)
        selection = lax.dynamic_index_in_dim(select, section_id, 0, keepdims=False)
        numerator = jnp.zeros((queries.shape[0], queries.shape[1]), jnp.float32)
        vote_count = jnp.zeros((queries.shape[0],), jnp.float32)
        for offset in range(1, 4):
            source = jnp.maximum(section_id - offset, 0).astype(jnp.int32)
            key_rows = lax.dynamic_index_in_dim(features, source, 0, keepdims=False)
            usable = jnp.where(section_id - offset >= 0, validity[source], 0).astype(jnp.float32)
            chosen = (selection // 2 ** (offset - 1) % 2).astype(jnp.float32) * usable
            warped = match_section(queries, key_rows)
            numerator = numerator + chosen[:, None] * offset_gain[offset - 1][None, :] * warped
            vote_count = vote_count + chosen
        return (numerator / jnp.maximum(vote_count, 1.0)[:, None]).astype(jnp.bfloat16)
    return lax.map(per_section, jnp.arange(SECTIONS, dtype=jnp.int32))
```

```python
import functools
import math

import jax
import jax.numpy as jnp
from jax import lax
from jax.experimental import pallas as pl
from jax.experimental.pallas import tpu as pltpu
from jax.sharding import PartitionSpec as P

score_factor = 2.5
offsets = 3
unusable = 32.0
usable_limit = 16.0
lanes = 128
row_block = 256
vmem = pl.BlockSpec(memory_space=pltpu.VMEM)
grant = pltpu.CompilerParams(vmem_limit_bytes=24 * 2**20)
smem = pl.BlockSpec(memory_space=pltpu.SMEM)


def from_behind(block, distance):
    n = lax.axis_size("sec")
    return lax.ppermute(block, "sec", [((i - distance) % n, i) for i in range(n)])


def from_partner(block, distance):
    return lax.ppermute(block, "tile", [(i ^ distance, i) for i in range(lax.axis_size("tile"))])


def prepare(select_ref, columns_ref):
    rows = jnp.broadcast_to(select_ref[...].astype(jnp.float32), (lanes, select_ref.shape[1]))
    columns_ref[...] = rows.T.astype(jnp.int32)


def fold(offset, first, last, scale, *refs):
    section_ref, query_ref, columns_ref, gain_ref, *refs = refs
    if not first:
        numerator_ref, count_ref, *refs = refs
    *key_refs, out_ref = refs[: len(refs) if last else -1]
    count_out_ref = None if last else refs[-1]
    num_rows, channels = query_ref.shape
    step = scale * math.log2(math.e)
    mark = key_refs[0][0:8, 0:lanes].astype(jnp.float32)[0:1, :]
    behind = (section_ref[0] >= offset).astype(jnp.float32)
    usable = jnp.where(mark <= usable_limit, behind, 0.0)
    gain = gain_ref[offset - 1 : offset, :]
    for row in range(0, num_rows, row_block):
        rows = slice(row, row + row_block)
        queries = query_ref[rows, :]
        scores = [
            lax.dot_general(
                queries, k[...], (((1,), (1,)), ((), ())), preferred_element_type=jnp.float32
            )
            for k in key_refs
        ]
        top = functools.reduce(jnp.maximum, [s.max(axis=1, keepdims=True) for s in scores]) * step
        total = 0.0
        weighted = 0.0
        for s, k in zip(scores, key_refs):
            weights = jnp.exp2(s * step - top)
            total = total + jnp.sum(weights, axis=1, keepdims=True)
            weighted = weighted + jnp.dot(
                weights.astype(jnp.bfloat16), k[...], preferred_element_type=jnp.float32
            )
        bits = (columns_ref[rows, :] >> (offset - 1)) & 1
        chosen = bits.astype(jnp.float32) * usable
        share = jnp.concatenate([chosen / total] * (channels // lanes), axis=1)
        numerator = weighted * share * gain
        count = chosen
        if not first:
            numerator = numerator + numerator_ref[rows, :]
            count = count + count_ref[rows, :]
        if last:
            divisor = jnp.concatenate([jnp.maximum(count, 1.0)] * (channels // lanes), axis=1)
            out_ref[rows, :] = (numerator / divisor).astype(jnp.bfloat16)
        else:
            out_ref[rows, :] = numerator
            count_out_ref[rows, :] = count


def shards(features, select, validity, offset_gain):
    queries = features[0]
    num_rows, channels = queries.shape
    scale = score_factor / math.sqrt(channels)
    section = lax.axis_index("sec").astype(jnp.int32)[None]
    columns = pl.pallas_call(
        prepare,
        out_shape=jax.ShapeDtypeStruct((num_rows, lanes), jnp.int32),
        in_specs=[vmem],
        out_specs=vmem,
        compiler_params=grant,
        name="prepare",
    )(select)
    sent = jnp.where(validity[0] != 0, queries, jnp.bfloat16(unusable))
    second = from_behind(sent, 2)
    first = from_behind(sent, 1)
    third = from_behind(second, 1)

    def all_tiles(tile):
        tiles = [tile]
        distance = lax.axis_size("tile") // 2
        while distance:
            tiles += [from_partner(t, distance) for t in tiles]
            distance //= 2
        return tiles

    state = []
    order = [(2, second), (1, first), (3, third)]
    for at, (offset, tile) in enumerate(order):
        last = at == len(order) - 1
        tiles = all_tiles(tile)
        keys = len(tiles) * num_rows
        wide = jax.ShapeDtypeStruct((num_rows, channels), jnp.bfloat16 if last else jnp.float32)
        narrow = jax.ShapeDtypeStruct((num_rows, lanes), jnp.float32)
        args = (section, queries, columns, offset_gain, *state, *tiles)
        state = pl.pallas_call(
            functools.partial(fold, offset, at == 0, last, scale),
            out_shape=wide if last else (wide, narrow),
            in_specs=[smem] + [vmem] * (len(args) - 1),
            out_specs=vmem if last else (vmem, vmem),
            cost_estimate=pl.CostEstimate(
                flops=4 * num_rows * keys * channels,
                transcendentals=num_rows * keys,
                bytes_accessed=2 * keys * channels,
            ),
            compiler_params=grant,
            name=f"fold{offset}",
        )(*args)
    return state[None]


def solution(mesh):
    in_specs = (P("sec", "tile", None), P("sec", "tile"), P("sec"), P())
    out_specs = P("sec", "tile", None)
    return jax.shard_map(shards, mesh=mesh, in_specs=in_specs, out_specs=out_specs, check_vma=False)
```

```python
import functools
import math

import jax
import jax.numpy as jnp
from jax import lax
from jax.experimental import pallas as pl
from jax.experimental.pallas import tpu as pltpu
from jax.sharding import PartitionSpec as P


score_factor = 2.5
unusable = 32.0
usable_limit = 16.0
lanes = 128
row_block = 256
vmem = pl.BlockSpec(memory_space=pltpu.VMEM)
smem = pl.BlockSpec(memory_space=pltpu.SMEM)
grant = pltpu.CompilerParams(vmem_limit_bytes=24 * 2**20)


def from_behind(block, distance):
    n = lax.axis_size("sec")
    return lax.ppermute(block, "sec", [((i - distance) % n, i) for i in range(n)])


def from_partner(block, distance):
    n = lax.axis_size("tile")
    return lax.ppermute(block, "tile", [(i ^ distance, i) for i in range(n)])


def widen(column, channels):
    return jnp.concatenate([column] * (channels // lanes), axis=1)


def is_usable(tile_ref):
    mark = tile_ref[0:8, 0:lanes].astype(jnp.float32)[0:1, :]
    return jnp.where(mark <= usable_limit, 1.0, 0.0)


def matched(queries, key_refs, scale):
    step = scale * math.log2(math.e)
    scores = [
        lax.dot_general(
            queries, k[...], (((1,), (1,)), ((), ())), preferred_element_type=jnp.float32
        )
        for k in key_refs
    ]
    top = functools.reduce(jnp.maximum, [s.max(axis=1, keepdims=True) for s in scores]) * step
    total = 0.0
    weighted = 0.0
    for s, k in zip(scores, key_refs):
        weights = jnp.exp2(s * step - top)
        total = total + jnp.sum(weights, axis=1, keepdims=True)
        weighted = weighted + jnp.dot(
            weights.astype(jnp.bfloat16), k[...], preferred_element_type=jnp.float32
        )
    return weighted, total


def chosen_rows(columns, offset, section_ref, usable):
    behind = (section_ref[0] >= offset).astype(jnp.float32)
    bits = (columns >> (offset - 1)) & 1
    return bits.astype(jnp.float32) * (usable * behind)


def prepare(select_ref, columns_ref):
    rows = jnp.broadcast_to(select_ref[...].astype(jnp.float32), (lanes, select_ref.shape[1]))
    columns_ref[...] = rows.T.astype(jnp.int32)


def answer(scale, query_ref, *refs):
    *key_refs, out_ref = refs
    num_rows, channels = query_ref.shape
    keep = widen(is_usable(key_refs[0]), channels) > 0.5
    for row in range(0, num_rows, row_block):
        rows = slice(row, row + row_block)
        weighted, total = matched(query_ref[rows, :], key_refs, scale)
        out_ref[rows, :] = jnp.where(keep, weighted / total, unusable).astype(jnp.bfloat16)


def fold(offset, first, scale, section_ref, query_ref, columns_ref, gain_ref, *refs):
    if not first:
        numerator_ref, count_ref, *refs = refs
    *key_refs, out_ref, count_out_ref = refs
    num_rows, channels = query_ref.shape
    usable = is_usable(key_refs[0])
    gain = gain_ref[offset - 1 : offset, :]
    for row in range(0, num_rows, row_block):
        rows = slice(row, row + row_block)
        weighted, total = matched(query_ref[rows, :], key_refs, scale)
        count = chosen_rows(columns_ref[rows, :], offset, section_ref, usable)
        numerator = weighted * widen(count / total, channels) * gain
        if not first:
            numerator = numerator + numerator_ref[rows, :]
            count = count + count_ref[rows, :]
        out_ref[rows, :] = numerator
        count_out_ref[rows, :] = count


def finish(
    offset, section_ref, columns_ref, gain_ref, numerator_ref, count_ref, warped_ref, out_ref
):
    _, channels = warped_ref.shape
    usable = is_usable(warped_ref)
    gain = gain_ref[offset - 1 : offset, :]
    chosen = chosen_rows(columns_ref[...], offset, section_ref, usable)
    divisor = jnp.maximum(count_ref[...] + chosen, 1.0)
    numerator = numerator_ref[...] + (
        warped_ref[...].astype(jnp.float32) * widen(chosen, channels) * gain
    )
    out_ref[...] = (numerator / widen(divisor, channels)).astype(jnp.bfloat16)


def shards(features, select, validity, offset_gain):
    queries = features[0]
    num_rows, channels = queries.shape
    scale = score_factor / math.sqrt(channels)
    section = lax.axis_index("sec").astype(jnp.int32)[None]
    wide = jax.ShapeDtypeStruct((num_rows, channels), jnp.float32)
    tile = jax.ShapeDtypeStruct((num_rows, channels), jnp.bfloat16)
    narrow = jax.ShapeDtypeStruct((num_rows, lanes), jnp.float32)
    keys = num_rows * lax.axis_size("tile")
    heavy = pl.CostEstimate(
        flops=4 * num_rows * keys * channels,
        transcendentals=num_rows * keys,
        bytes_accessed=2 * keys * channels,
    )

    def call(body, out, args, cost=None, scalars=0):
        return pl.pallas_call(
            body,
            out_shape=out,
            in_specs=[smem] * scalars + [vmem] * (len(args) - scalars),
            out_specs=jax.tree.map(lambda _: vmem, out),
            cost_estimate=cost,
            compiler_params=grant,
        )(*args)

    def all_tiles(t):
        tiles = [t]
        distance = lax.axis_size("tile") // 2
        while distance:
            for held in tuple(tiles):
                tiles.append(from_partner(held, distance))
            distance //= 2
        return tiles

    columns_shape = jax.ShapeDtypeStruct((num_rows, lanes), jnp.int32)
    columns = call(prepare, columns_shape, (select,))
    sent = jnp.where(validity[0] != 0, queries, jnp.bfloat16(unusable))
    second = from_behind(sent, 2)
    first = from_behind(sent, 1)
    ahead = from_behind(queries, -1)
    second_tiles = all_tiles(second)
    first_tiles = all_tiles(first)
    answered = call(functools.partial(answer, scale), tile, (ahead, *second_tiles), heavy)
    third = from_behind(answered, 1)
    common = (section, queries, columns, offset_gain)
    state = call(
        functools.partial(fold, 2, True, scale), (wide, narrow), (*common, *second_tiles), heavy, 1
    )
    state = call(
        functools.partial(fold, 1, False, scale),
        (wide, narrow),
        (*common, *state, *first_tiles),
        heavy,
        1,
    )
    out = call(
        functools.partial(finish, 3),
        tile,
        (section, columns, offset_gain, *state, third),
        scalars=1,
    )
    return out[None]


def solution(mesh):
    in_specs = (P("sec", "tile", None), P("sec", "tile"), P("sec"), P())
    out_specs = P("sec", "tile", None)

    def step(*arrays):
        return shards(*arrays)

    step = jax.shard_map(step, mesh=mesh, in_specs=in_specs, out_specs=out_specs, check_vma=False)
    return step
```

```python
import functools
import math

import jax
import jax.numpy as jnp
from jax import lax
from jax.experimental import pallas as pl
from jax.experimental.pallas import tpu as pltpu
from jax.sharding import PartitionSpec as P


score_factor = 2.5
unusable = 32.0
usable_limit = 16.0
lanes = 128
sublanes = 8
row_block = 256
vmem = pl.BlockSpec(memory_space=pltpu.VMEM)
smem = pl.BlockSpec(memory_space=pltpu.SMEM)
grant = pltpu.CompilerParams(vmem_limit_bytes=24 * 2**20)


def from_behind(block, distance):
    n = lax.axis_size("sec")
    return lax.ppermute(block, "sec", [((i - distance) % n, i) for i in range(n)])


def swapped(block, first):
    pairs = [(i, i + 1) for i in range(first, lax.axis_size("sec") - 1, 2)]
    return lax.ppermute(block, "sec", pairs + [(j, i) for i, j in pairs])


def from_partner(block, distance):
    n = lax.axis_size("tile")
    return lax.ppermute(block, "tile", [(i ^ distance, i) for i in range(n)])


def widen(column, channels):
    return jnp.concatenate([column] * (channels // lanes), axis=1)


def is_usable(tile_ref):
    mark = tile_ref[0:8, 0:lanes].astype(jnp.float32)[0:1, :]
    return jnp.where(mark <= usable_limit, 1.0, 0.0)


def matched(queries, key_refs, scale):
    step = scale * math.log2(math.e)
    scores = [
        lax.dot_general(
            queries, k[...], (((1,), (1,)), ((), ())), preferred_element_type=jnp.float32
        )
        for k in key_refs
    ]
    top = functools.reduce(jnp.maximum, [s.max(axis=1, keepdims=True) for s in scores]) * step
    total = 0.0
    weighted = 0.0
    for s, k in zip(scores, key_refs):
        weights = jnp.exp2(s * step - top)
        total = total + jnp.sum(weights, axis=1, keepdims=True)
        weighted = weighted + jnp.dot(
            weights.astype(jnp.bfloat16), k[...], preferred_element_type=jnp.float32
        )
    return weighted, total


def chosen_rows(columns, offset, section_ref, usable):
    behind = (section_ref[0] >= offset).astype(jnp.float32)
    bits = (columns >> (offset - 1)) & 1
    return bits.astype(jnp.float32) * (usable * behind)


def prepare(select_ref, validity_ref, columns_ref, mark_ref):
    mark_ref[...] = jnp.broadcast_to(validity_ref[...].astype(jnp.float32), mark_ref.shape)
    rows = jnp.broadcast_to(select_ref[...].astype(jnp.float32), (lanes, select_ref.shape[1]))
    columns_ref[...] = rows.T.astype(jnp.int32)


def answer(scale, num_sections, section_ref, flag_ref, beside_ref, across_ref, *refs):
    *key_refs, out_ref = refs
    num_rows, channels = out_ref.shape
    section = section_ref[0]
    needed = (section >= 2) & (section < num_sections - 1)

    @pl.when(needed)
    def _():
        keep = jnp.broadcast_to(widen(flag_ref[0:1, :], channels), (row_block, channels)) > 0.5
        for row in range(0, num_rows, row_block):
            rows = slice(row, row + row_block)
            queries = jnp.where(section % 2 == 1, across_ref[rows, :], beside_ref[rows, :])
            weighted, total = matched(queries, key_refs, scale)
            out_ref[rows, :] = jnp.where(keep, weighted / total, unusable).astype(jnp.bfloat16)

    @pl.when(jnp.logical_not(needed))
    def _():
        out_ref[...] = jnp.full(out_ref.shape, unusable, jnp.bfloat16)


def fold(offset, first, scale, section_ref, flag_ref, query_ref, columns_ref, gain_ref, *refs):
    if not first:
        numerator_ref, count_ref, *refs = refs
    *key_refs, out_ref, count_out_ref = refs
    num_rows, channels = query_ref.shape
    usable = flag_ref[0:1, :]
    gain = gain_ref[offset - 1 : offset, :]
    needed = section_ref[0] >= offset

    @pl.when(needed)
    def _():
        for row in range(0, num_rows, row_block):
            rows = slice(row, row + row_block)
            weighted, total = matched(query_ref[rows, :], key_refs, scale)
            count = chosen_rows(columns_ref[rows, :], offset, section_ref, usable)
            numerator = weighted * widen(count / total, channels) * gain
            if not first:
                numerator = numerator + numerator_ref[rows, :]
                count = count + count_ref[rows, :]
            out_ref[rows, :] = numerator
            count_out_ref[rows, :] = count

    @pl.when(jnp.logical_not(needed))
    def _():
        if first:
            out_ref[...] = jnp.zeros_like(out_ref)
            count_out_ref[...] = jnp.zeros_like(count_out_ref)
        else:
            out_ref[...] = numerator_ref[...]
            count_out_ref[...] = count_ref[...]


def finish(
    offset, section_ref, columns_ref, gain_ref, numerator_ref, count_ref, warped_ref, out_ref
):
    _, channels = warped_ref.shape
    usable = is_usable(warped_ref)
    gain = gain_ref[offset - 1 : offset, :]
    chosen = chosen_rows(columns_ref[...], offset, section_ref, usable)
    divisor = jnp.maximum(count_ref[...] + chosen, 1.0)
    numerator = numerator_ref[...] + (
        warped_ref[...].astype(jnp.float32) * widen(chosen, channels) * gain
    )
    out_ref[...] = (numerator / widen(divisor, channels)).astype(jnp.bfloat16)


def shards(features, select, validity, offset_gain):
    queries = features[0]
    num_rows, channels = queries.shape
    scale = score_factor / math.sqrt(channels)
    section = lax.axis_index("sec").astype(jnp.int32)[None]
    wide = jax.ShapeDtypeStruct((num_rows, channels), jnp.float32)
    tile = jax.ShapeDtypeStruct((num_rows, channels), jnp.bfloat16)
    narrow = jax.ShapeDtypeStruct((num_rows, lanes), jnp.float32)
    keys = num_rows * lax.axis_size("tile")
    heavy = pl.CostEstimate(
        flops=4 * num_rows * keys * channels,
        transcendentals=num_rows * keys,
        bytes_accessed=2 * keys * channels,
    )

    def call(body, out, args, cost=None, scalars=0):
        return pl.pallas_call(
            body,
            out_shape=out,
            in_specs=[smem] * scalars + [vmem] * (len(args) - scalars),
            out_specs=jax.tree.map(lambda _: vmem, out),
            cost_estimate=cost,
            compiler_params=grant,
        )(*args)

    def all_tiles(t):
        tiles = [t]
        distance = lax.axis_size("tile") // 2
        while distance:
            for held in tuple(tiles):
                tiles.append(from_partner(held, distance))
            distance //= 2
        return tiles

    columns_shape = jax.ShapeDtypeStruct((num_rows, lanes), jnp.int32)
    mark_shape = jax.ShapeDtypeStruct((sublanes, lanes), jnp.float32)
    columns, mark = call(prepare, (columns_shape, mark_shape), (select, validity[:, None]))
    second = from_behind(queries, 2)
    beside = swapped(queries, 0)
    across = swapped(queries, 1)
    flag1 = from_behind(mark, 1)
    flag2 = from_behind(mark, 2)
    first = jnp.where(section[0] % 2 == 1, beside, across)
    second_tiles = all_tiles(second)
    first_tiles = all_tiles(first)
    answered = call(
        functools.partial(answer, scale, lax.axis_size("sec")),
        tile,
        (section, flag2, beside, across, *second_tiles),
        heavy,
        1,
    )
    third = from_behind(answered, 1)
    common = (queries, columns, offset_gain)
    state = call(
        functools.partial(fold, 2, True, scale),
        (wide, narrow),
        (section, flag2, *common, *second_tiles),
        heavy,
        1,
    )
    state = call(
        functools.partial(fold, 1, False, scale),
        (wide, narrow),
        (section, flag1, *common, *state, *first_tiles),
        heavy,
        1,
    )
    out = call(
        functools.partial(finish, 3),
        tile,
        (section, columns, offset_gain, *state, third),
        scalars=1,
    )
    return out[None]


def solution(mesh):
    in_specs = (P("sec", "tile", None), P("sec", "tile"), P("sec"), P())
    out_specs = P("sec", "tile", None)

    def step(*arrays):
        return shards(*arrays)

    step = jax.shard_map(step, mesh=mesh, in_specs=in_specs, out_specs=out_specs, check_vma=False)
    return step
```

```python
import functools
import math

import jax
import jax.numpy as jnp
from jax import lax
from jax.experimental import pallas as pl
from jax.experimental.pallas import tpu as pltpu
from jax.sharding import PartitionSpec as P


score_factor = 2.5
unusable = 32.0
usable_limit = 16.0
lanes = 128
sublanes = 8
row_block = 256
vmem = pl.BlockSpec(memory_space=pltpu.VMEM)
smem = pl.BlockSpec(memory_space=pltpu.SMEM)
grant = pltpu.CompilerParams(vmem_limit_bytes=24 * 2**20)


def from_behind(block, distance):
    n = lax.axis_size("sec")
    return lax.ppermute(block, "sec", [((i - distance) % n, i) for i in range(n)])


def swapped(block, first):
    pairs = [(i, i + 1) for i in range(first, lax.axis_size("sec") - 1, 2)]
    return lax.ppermute(block, "sec", pairs + [(j, i) for i, j in pairs])


def from_partner(block, distance):
    n = lax.axis_size("tile")
    return lax.ppermute(block, "tile", [(i ^ distance, i) for i in range(n)])


def widen(column, channels):
    return jnp.concatenate([column] * (channels // lanes), axis=1)


def is_usable(tile_ref):
    mark = tile_ref[0:8, 0:lanes].astype(jnp.float32)[0:1, :]
    return jnp.where(mark <= usable_limit, 1.0, 0.0)


def matched(queries, key_refs, scale):
    step = scale * math.log2(math.e)
    scores = [
        lax.dot_general(
            queries, k[...], (((1,), (1,)), ((), ())), preferred_element_type=jnp.float32
        )
        for k in key_refs
    ]
    top = functools.reduce(jnp.maximum, [s.max(axis=1, keepdims=True) for s in scores]) * step
    total = 0.0
    weighted = 0.0
    for s, k in zip(scores, key_refs):
        weights = jnp.exp2(s * step - top)
        total = total + jnp.sum(weights, axis=1, keepdims=True)
        weighted = weighted + jnp.dot(
            weights.astype(jnp.bfloat16), k[...], preferred_element_type=jnp.float32
        )
    return weighted, total


def chosen_rows(columns, offset, section_ref, usable):
    behind = (section_ref[0] >= offset).astype(jnp.float32)
    bits = (columns >> (offset - 1)) & 1
    return bits.astype(jnp.float32) * (usable * behind)


def note(validity_ref, mark_ref):
    mark_ref[...] = jnp.broadcast_to(validity_ref[...].astype(jnp.float32), mark_ref.shape)


def prepare(select_ref, columns_ref):
    rows = jnp.broadcast_to(select_ref[...].astype(jnp.float32), (lanes, select_ref.shape[1]))
    columns_ref[...] = rows.T.astype(jnp.int32)


def answer(scale, num_sections, section_ref, flag_ref, beside_ref, across_ref, *refs):
    *key_refs, out_ref = refs
    num_rows, channels = out_ref.shape
    section = section_ref[0]
    needed = (section >= 2) & (section < num_sections - 1)

    @pl.when(needed)
    def _():
        keep = jnp.broadcast_to(widen(flag_ref[0:1, :], channels), (row_block, channels)) > 0.5
        for row in range(0, num_rows, row_block):
            rows = slice(row, row + row_block)
            queries = jnp.where(section % 2 == 1, across_ref[rows, :], beside_ref[rows, :])
            weighted, total = matched(queries, key_refs, scale)
            out_ref[rows, :] = jnp.where(keep, weighted / total, unusable).astype(jnp.bfloat16)

    @pl.when(jnp.logical_not(needed))
    def _():
        out_ref[...] = jnp.full(out_ref.shape, unusable, jnp.bfloat16)


def fold(offset, first, scale, section_ref, flag_ref, query_ref, columns_ref, gain_ref, *refs):
    if not first:
        numerator_ref, count_ref, *refs = refs
    *key_refs, out_ref, count_out_ref = refs
    num_rows, channels = query_ref.shape
    usable = flag_ref[0:1, :]
    gain = gain_ref[offset - 1 : offset, :]
    needed = section_ref[0] >= offset

    @pl.when(needed)
    def _():
        for row in range(0, num_rows, row_block):
            rows = slice(row, row + row_block)
            weighted, total = matched(query_ref[rows, :], key_refs, scale)
            count = chosen_rows(columns_ref[rows, :], offset, section_ref, usable)
            numerator = weighted * widen(count / total, channels) * gain
            if not first:
                numerator = numerator + numerator_ref[rows, :]
                count = count + count_ref[rows, :]
            out_ref[rows, :] = numerator
            count_out_ref[rows, :] = count

    @pl.when(jnp.logical_not(needed))
    def _():
        if first:
            out_ref[...] = jnp.zeros_like(out_ref)
            count_out_ref[...] = jnp.zeros_like(count_out_ref)
        else:
            out_ref[...] = numerator_ref[...]
            count_out_ref[...] = count_ref[...]


def finish(
    offset, section_ref, columns_ref, gain_ref, numerator_ref, count_ref, warped_ref, out_ref
):
    _, channels = warped_ref.shape
    usable = is_usable(warped_ref)
    gain = gain_ref[offset - 1 : offset, :]
    chosen = chosen_rows(columns_ref[...], offset, section_ref, usable)
    divisor = jnp.maximum(count_ref[...] + chosen, 1.0)
    numerator = numerator_ref[...] + (
        warped_ref[...].astype(jnp.float32) * widen(chosen, channels) * gain
    )
    out_ref[...] = (numerator / widen(divisor, channels)).astype(jnp.bfloat16)


def shards(features, select, validity, offset_gain):
    queries = features[0]
    num_rows, channels = queries.shape
    scale = score_factor / math.sqrt(channels)
    section = lax.axis_index("sec").astype(jnp.int32)[None]
    wide = jax.ShapeDtypeStruct((num_rows, channels), jnp.float32)
    tile = jax.ShapeDtypeStruct((num_rows, channels), jnp.bfloat16)
    narrow = jax.ShapeDtypeStruct((num_rows, lanes), jnp.float32)
    keys = num_rows * lax.axis_size("tile")
    heavy = pl.CostEstimate(
        flops=4 * num_rows * keys * channels,
        transcendentals=num_rows * keys,
        bytes_accessed=2 * keys * channels,
    )

    def call(body, out, args, cost=None, scalars=0):
        return pl.pallas_call(
            body,
            out_shape=out,
            in_specs=[smem] * scalars + [vmem] * (len(args) - scalars),
            out_specs=jax.tree.map(lambda _: vmem, out),
            cost_estimate=cost,
            compiler_params=grant,
        )(*args)

    def all_tiles(t):
        tiles = [t]
        distance = lax.axis_size("tile") // 2
        while distance:
            for held in tuple(tiles):
                tiles.append(from_partner(held, distance))
            distance //= 2
        return tiles

    columns_shape = jax.ShapeDtypeStruct((num_rows, lanes), jnp.int32)
    mark_shape = jax.ShapeDtypeStruct((sublanes, lanes), jnp.float32)
    columns = call(prepare, columns_shape, (select,))
    mark = call(note, mark_shape, (validity[:, None],))
    second = from_behind(queries, 2)
    beside = swapped(queries, 0)
    across = swapped(queries, 1)
    flag1 = from_behind(mark, 1)
    flag2 = from_behind(mark, 2)
    first = jnp.where(section[0] % 2 == 1, beside, across)
    second_tiles = all_tiles(second)
    first_tiles = all_tiles(first)
    answered = call(
        functools.partial(answer, scale, lax.axis_size("sec")),
        tile,
        (section, flag2, beside, across, *second_tiles),
        heavy,
        1,
    )
    n = lax.axis_size("sec")
    routes = [(i, i + 1) for i in range(2, n - 1)] + [(0, 2), (1, 0), (n - 1, 1)]
    third = lax.ppermute(answered, "sec", routes)
    common = (queries, columns, offset_gain)
    state = call(
        functools.partial(fold, 2, True, scale),
        (wide, narrow),
        (section, flag2, *common, *second_tiles),
        heavy,
        1,
    )
    state = call(
        functools.partial(fold, 1, False, scale),
        (wide, narrow),
        (section, flag1, *common, *state, *first_tiles),
        heavy,
        1,
    )
    out = call(
        functools.partial(finish, 3),
        tile,
        (section, columns, offset_gain, *state, third),
        scalars=1,
    )
    return out[None]


def solution(mesh):
    in_specs = (P("sec", "tile", None), P("sec", "tile"), P("sec"), P())
    out_specs = P("sec", "tile", None)

    def step(*arrays):
        return shards(*arrays)

    step = jax.shard_map(step, mesh=mesh, in_specs=in_specs, out_specs=out_specs, check_vma=False)
    return step
```

```python
import functools
import math

import jax
import jax.numpy as jnp
from jax import lax
from jax.experimental import pallas as pl
from jax.experimental.pallas import tpu as pltpu
from jax.sharding import PartitionSpec as P


score_factor = 2.5
unusable = 32.0
usable_limit = 16.0
lanes = 128
sublanes = 8
row_block = 256
vmem = pl.BlockSpec(memory_space=pltpu.VMEM)
smem = pl.BlockSpec(memory_space=pltpu.SMEM)
grant = pltpu.CompilerParams(vmem_limit_bytes=24 * 2**20)


def from_behind(block, distance):
    n = lax.axis_size("sec")
    return lax.ppermute(block, "sec", [((i - distance) % n, i) for i in range(n)])


def swapped(block, first):
    pairs = [(i, i + 1) for i in range(first, lax.axis_size("sec") - 1, 2)]
    return lax.ppermute(block, "sec", pairs + [(j, i) for i, j in pairs])


def from_partner(block, distance):
    n = lax.axis_size("tile")
    return lax.ppermute(block, "tile", [(i ^ distance, i) for i in range(n)])


def widen(column, channels):
    return jnp.concatenate([column] * (channels // lanes), axis=1)


def is_usable(tile_ref):
    mark = tile_ref[0:8, 0:lanes].astype(jnp.float32)[0:1, :]
    return jnp.where(mark <= usable_limit, 1.0, 0.0)


def matched(query_rows, key_refs, scale, num_rows):
    step = scale * math.log2(math.e)
    blocks = [slice(row, row + row_block) for row in range(0, num_rows, row_block)]

    def scored(rows):
        queries = query_rows(rows)
        return [
            lax.dot_general(
                queries, k[...], (((1,), (1,)), ((), ())), preferred_element_type=jnp.float32
            )
            for k in key_refs
        ]

    scores = scored(blocks[0])
    for rows, rows_after in zip(blocks, blocks[1:] + [None]):
        scores_after = None if rows_after is None else scored(rows_after)
        top = functools.reduce(jnp.maximum, [s.max(axis=1, keepdims=True) for s in scores]) * step
        total = 0.0
        weighted = 0.0
        for s, k in zip(scores, key_refs):
            weights = jnp.exp2(s * step - top)
            total = total + jnp.sum(weights, axis=1, keepdims=True)
            weighted = weighted + jnp.dot(
                weights.astype(jnp.bfloat16), k[...], preferred_element_type=jnp.float32
            )
        yield rows, weighted, total
        scores = scores_after


def chosen_rows(columns, offset, section_ref, usable):
    behind = (section_ref[0] >= offset).astype(jnp.float32)
    bits = (columns >> (offset - 1)) & 1
    return bits.astype(jnp.float32) * (usable * behind)


def note(validity_ref, mark_ref):
    mark_ref[...] = jnp.broadcast_to(validity_ref[...].astype(jnp.float32), mark_ref.shape)


def prepare(select_ref, columns_ref):
    rows = jnp.broadcast_to(select_ref[...].astype(jnp.float32), (lanes, select_ref.shape[1]))
    columns_ref[...] = rows.T.astype(jnp.int32)


def answer(scale, num_sections, section_ref, flag_ref, beside_ref, across_ref, *refs):
    *key_refs, out_ref = refs
    num_rows, channels = out_ref.shape
    section = section_ref[0]
    needed = (section >= 2) & (section < num_sections - 1)

    @pl.when(needed)
    def _():
        keep = jnp.broadcast_to(widen(flag_ref[0:1, :], channels), (row_block, channels)) > 0.5

        def queries(rows):
            return jnp.where(section % 2 == 1, across_ref[rows, :], beside_ref[rows, :])

        for rows, weighted, total in matched(queries, key_refs, scale, num_rows):
            out_ref[rows, :] = jnp.where(keep, weighted / total, unusable).astype(jnp.bfloat16)

    @pl.when(jnp.logical_not(needed))
    def _():
        out_ref[...] = jnp.full(out_ref.shape, unusable, jnp.bfloat16)


def fold(offset, first, scale, section_ref, flag_ref, query_ref, columns_ref, gain_ref, *refs):
    if not first:
        numerator_ref, count_ref, *refs = refs
    *key_refs, out_ref, count_out_ref = refs
    num_rows, channels = query_ref.shape
    usable = flag_ref[0:1, :]
    gain = gain_ref[offset - 1 : offset, :]
    needed = section_ref[0] >= offset

    @pl.when(needed)
    def _():
        for rows, weighted, total in matched(lambda r: query_ref[r, :], key_refs, scale, num_rows):
            count = chosen_rows(columns_ref[rows, :], offset, section_ref, usable)
            numerator = weighted * widen(count / total, channels) * gain
            if not first:
                numerator = numerator + numerator_ref[rows, :]
                count = count + count_ref[rows, :]
            out_ref[rows, :] = numerator
            count_out_ref[rows, :] = count

    @pl.when(jnp.logical_not(needed))
    def _():
        if first:
            out_ref[...] = jnp.zeros_like(out_ref)
            count_out_ref[...] = jnp.zeros_like(count_out_ref)
        else:
            out_ref[...] = numerator_ref[...]
            count_out_ref[...] = count_ref[...]


def finish(
    offset, section_ref, columns_ref, gain_ref, numerator_ref, count_ref, warped_ref, out_ref
):
    _, channels = warped_ref.shape
    usable = is_usable(warped_ref)
    gain = gain_ref[offset - 1 : offset, :]
    chosen = chosen_rows(columns_ref[...], offset, section_ref, usable)
    divisor = jnp.maximum(count_ref[...] + chosen, 1.0)
    numerator = numerator_ref[...] + (
        warped_ref[...].astype(jnp.float32) * widen(chosen, channels) * gain
    )
    out_ref[...] = (numerator / widen(divisor, channels)).astype(jnp.bfloat16)


def shards(features, select, validity, offset_gain):
    queries = features[0]
    num_rows, channels = queries.shape
    scale = score_factor / math.sqrt(channels)
    section = lax.axis_index("sec").astype(jnp.int32)[None]
    wide = jax.ShapeDtypeStruct((num_rows, channels), jnp.float32)
    tile = jax.ShapeDtypeStruct((num_rows, channels), jnp.bfloat16)
    narrow = jax.ShapeDtypeStruct((num_rows, lanes), jnp.float32)
    keys = num_rows * lax.axis_size("tile")
    heavy = pl.CostEstimate(
        flops=4 * num_rows * keys * channels,
        transcendentals=num_rows * keys,
        bytes_accessed=2 * keys * channels,
    )

    def call(body, out, args, cost=None, scalars=0):
        return pl.pallas_call(
            body,
            out_shape=out,
            in_specs=[smem] * scalars + [vmem] * (len(args) - scalars),
            out_specs=jax.tree.map(lambda _: vmem, out),
            cost_estimate=cost,
            compiler_params=grant,
        )(*args)

    def all_tiles(t):
        tiles = [t]
        distance = lax.axis_size("tile") // 2
        while distance:
            for held in tuple(tiles):
                tiles.append(from_partner(held, distance))
            distance //= 2
        return tiles

    columns_shape = jax.ShapeDtypeStruct((num_rows, lanes), jnp.int32)
    mark_shape = jax.ShapeDtypeStruct((sublanes, lanes), jnp.float32)
    columns = call(prepare, columns_shape, (select,))
    mark = call(note, mark_shape, (validity[:, None],))
    second = from_behind(queries, 2)
    beside = swapped(queries, 0)
    across = swapped(queries, 1)
    flag1 = from_behind(mark, 1)
    flag2 = from_behind(mark, 2)
    first = jnp.where(section[0] % 2 == 1, beside, across)
    second_tiles = all_tiles(second)
    first_tiles = all_tiles(first)
    answered = call(
        functools.partial(answer, scale, lax.axis_size("sec")),
        tile,
        (section, flag2, beside, across, *second_tiles),
        heavy,
        1,
    )
    n = lax.axis_size("sec")
    routes = [(i, i + 1) for i in range(2, n - 1)] + [(0, 2), (1, 0), (n - 1, 1)]
    third = lax.ppermute(answered, "sec", routes)
    common = (queries, columns, offset_gain)
    state = call(
        functools.partial(fold, 2, True, scale),
        (wide, narrow),
        (section, flag2, *common, *second_tiles),
        heavy,
        1,
    )
    state = call(
        functools.partial(fold, 1, False, scale),
        (wide, narrow),
        (section, flag1, *common, *state, *first_tiles),
        heavy,
        1,
    )
    out = call(
        functools.partial(finish, 3),
        tile,
        (section, columns, offset_gain, *state, third),
        scalars=1,
    )
    return out[None]


def solution(mesh):
    in_specs = (P("sec", "tile", None), P("sec", "tile"), P("sec"), P())
    out_specs = P("sec", "tile", None)

    def step(*arrays):
        return shards(*arrays)

    step = jax.shard_map(step, mesh=mesh, in_specs=in_specs, out_specs=out_specs, check_vma=False)
    return step
```

```python
import functools
import math

import jax
import jax.numpy as jnp
from jax import lax
from jax.experimental import pallas as pl
from jax.experimental.pallas import tpu as pltpu
from jax.sharding import PartitionSpec as P


score_factor = 2.5
unusable = 32.0
usable_limit = 16.0
lanes = 128
sublanes = 8
row_block = 256
vmem = pl.BlockSpec(memory_space=pltpu.VMEM)
smem = pl.BlockSpec(memory_space=pltpu.SMEM)
grant = pltpu.CompilerParams(vmem_limit_bytes=24 * 2**20)


def from_behind(block, distance):
    n = lax.axis_size("sec")
    return lax.ppermute(block, "sec", [((i - distance) % n, i) for i in range(n)])


def over_both(block, route):
    n, tiles = lax.axis_size("sec"), lax.axis_size("tile")
    pairs = []
    for i in range(n):
        for t in range(tiles):
            to_section, to_tile = route(i, t, n)
            pairs.append((i * tiles + t, to_section * tiles + to_tile))
    return lax.ppermute(block, ("sec", "tile"), pairs)


def up_and_down(block, parity):
    def route(i, t, n):
        to = i + 2 if t % 2 == parity else i - 2
        return (to, t) if 0 <= to < n else (i, t ^ 1)

    return over_both(block, route)


def swapped(block, first):
    def route(i, t, n):
        to = i + 1 if i % 2 == first else i - 1
        return (to, t) if 0 <= to < n else (i, t ^ 1)

    return over_both(block, route)


def from_partner(block, distance):
    n = lax.axis_size("tile")
    return lax.ppermute(block, "tile", [(i ^ distance, i) for i in range(n)])


def widen(column, channels):
    return jnp.concatenate([column] * (channels // lanes), axis=1)


def is_usable(tile_ref):
    mark = tile_ref[0:8, 0:lanes].astype(jnp.float32)[0:1, :]
    return jnp.where(mark <= usable_limit, 1.0, 0.0)


def matched(query_rows, key_refs, scale, num_rows):
    step = scale * math.log2(math.e)
    blocks = [slice(row, row + row_block) for row in range(0, num_rows, row_block)]

    def scored(rows):
        queries = query_rows(rows)
        return [
            lax.dot_general(
                queries, k[...], (((1,), (1,)), ((), ())), preferred_element_type=jnp.float32
            )
            for k in key_refs
        ]

    scores = scored(blocks[0])
    for rows, rows_after in zip(blocks, blocks[1:] + [None]):
        scores_after = None if rows_after is None else scored(rows_after)
        top = functools.reduce(jnp.maximum, [s.max(axis=1, keepdims=True) for s in scores]) * step
        total = 0.0
        weighted = 0.0
        for s, k in zip(scores, key_refs):
            weights = jnp.exp2(s * step - top)
            total = total + jnp.sum(weights, axis=1, keepdims=True)
            weighted = weighted + jnp.dot(
                weights.astype(jnp.bfloat16), k[...], preferred_element_type=jnp.float32
            )
        yield rows, weighted, total
        scores = scores_after


def chosen_rows(columns, offset, section_ref, usable):
    behind = (section_ref[0] >= offset).astype(jnp.float32)
    bits = (columns >> (offset - 1)) & 1
    return bits.astype(jnp.float32) * (usable * behind)


def note(validity_ref, mark_ref):
    mark_ref[...] = jnp.broadcast_to(validity_ref[...].astype(jnp.float32), mark_ref.shape)


def prepare(select_ref, columns_ref):
    rows = jnp.broadcast_to(select_ref[...].astype(jnp.float32), (lanes, select_ref.shape[1]))
    columns_ref[...] = rows.T.astype(jnp.int32)


def answer(scale, num_sections, section_ref, flag_ref, beside_ref, across_ref, *refs):
    *key_refs, out_ref = refs
    num_rows, channels = out_ref.shape
    section = section_ref[0]
    needed = (section >= 2) & (section < num_sections - 1)

    @pl.when(needed)
    def _():
        keep = jnp.broadcast_to(widen(flag_ref[0:1, :], channels), (row_block, channels)) > 0.5

        def queries(rows):
            return jnp.where(section % 2 == 1, across_ref[rows, :], beside_ref[rows, :])

        for rows, weighted, total in matched(queries, key_refs, scale, num_rows):
            out_ref[rows, :] = jnp.where(keep, weighted / total, unusable).astype(jnp.bfloat16)

    @pl.when(jnp.logical_not(needed))
    def _():
        out_ref[...] = jnp.full(out_ref.shape, unusable, jnp.bfloat16)


def fold(offset, first, scale, section_ref, flag_ref, query_ref, columns_ref, gain_ref, *refs):
    if not first:
        numerator_ref, count_ref, *refs = refs
    *key_refs, out_ref, count_out_ref = refs
    num_rows, channels = query_ref.shape
    usable = flag_ref[0:1, :]
    gain = gain_ref[offset - 1 : offset, :]
    needed = section_ref[0] >= offset

    @pl.when(needed)
    def _():
        for rows, weighted, total in matched(lambda r: query_ref[r, :], key_refs, scale, num_rows):
            count = chosen_rows(columns_ref[rows, :], offset, section_ref, usable)
            numerator = weighted * widen(count / total, channels) * gain
            if not first:
                numerator = numerator + numerator_ref[rows, :]
                count = count + count_ref[rows, :]
            out_ref[rows, :] = numerator
            count_out_ref[rows, :] = count

    @pl.when(jnp.logical_not(needed))
    def _():
        if first:
            out_ref[...] = jnp.zeros_like(out_ref)
            count_out_ref[...] = jnp.zeros_like(count_out_ref)
        else:
            out_ref[...] = numerator_ref[...]
            count_out_ref[...] = count_ref[...]


def finish(
    offset, section_ref, columns_ref, gain_ref, numerator_ref, count_ref, warped_ref, out_ref
):
    _, channels = warped_ref.shape
    usable = is_usable(warped_ref)
    gain = gain_ref[offset - 1 : offset, :]
    chosen = chosen_rows(columns_ref[...], offset, section_ref, usable)
    divisor = jnp.maximum(count_ref[...] + chosen, 1.0)
    numerator = numerator_ref[...] + (
        warped_ref[...].astype(jnp.float32) * widen(chosen, channels) * gain
    )
    out_ref[...] = (numerator / widen(divisor, channels)).astype(jnp.bfloat16)


def shards(features, select, validity, offset_gain):
    queries = features[0]
    num_rows, channels = queries.shape
    scale = score_factor / math.sqrt(channels)
    section = lax.axis_index("sec").astype(jnp.int32)[None]
    wide = jax.ShapeDtypeStruct((num_rows, channels), jnp.float32)
    tile = jax.ShapeDtypeStruct((num_rows, channels), jnp.bfloat16)
    narrow = jax.ShapeDtypeStruct((num_rows, lanes), jnp.float32)
    keys = num_rows * lax.axis_size("tile")
    heavy = pl.CostEstimate(
        flops=4 * num_rows * keys * channels,
        transcendentals=num_rows * keys,
        bytes_accessed=2 * keys * channels,
    )

    def call(body, out, args, cost=None, scalars=0):
        return pl.pallas_call(
            body,
            out_shape=out,
            in_specs=[smem] * scalars + [vmem] * (len(args) - scalars),
            out_specs=jax.tree.map(lambda _: vmem, out),
            cost_estimate=cost,
            compiler_params=grant,
        )(*args)

    def all_tiles(t):
        tiles = [t]
        distance = lax.axis_size("tile") // 2
        while distance:
            for held in tuple(tiles):
                tiles.append(from_partner(held, distance))
            distance //= 2
        return tiles

    columns_shape = jax.ShapeDtypeStruct((num_rows, lanes), jnp.int32)
    mark_shape = jax.ShapeDtypeStruct((sublanes, lanes), jnp.float32)
    columns = call(prepare, columns_shape, (select,))
    mark = call(note, mark_shape, (validity[:, None],))
    even_up = up_and_down(queries, 0)
    odd_up = up_and_down(queries, 1)
    second = jnp.where(lax.axis_index("tile") % 2 == 0, even_up, odd_up)
    beside = swapped(queries, 0)
    across = swapped(queries, 1)
    flag1 = from_behind(mark, 1)
    flag2 = from_behind(mark, 2)
    first = jnp.where(section[0] % 2 == 1, beside, across)
    second_tiles = all_tiles(second)
    first_tiles = all_tiles(first)
    answered = call(
        functools.partial(answer, scale, lax.axis_size("sec")),
        tile,
        (section, flag2, beside, across, *second_tiles),
        heavy,
        1,
    )
    n = lax.axis_size("sec")
    routes = [(i, i + 1) for i in range(2, n - 1)] + [(0, 2), (1, 0), (n - 1, 1)]
    third = lax.ppermute(answered, "sec", routes)
    common = (queries, columns, offset_gain)
    state = call(
        functools.partial(fold, 2, True, scale),
        (wide, narrow),
        (section, flag2, *common, *second_tiles),
        heavy,
        1,
    )
    state = call(
        functools.partial(fold, 1, False, scale),
        (wide, narrow),
        (section, flag1, *common, *state, *first_tiles),
        heavy,
        1,
    )
    out = call(
        functools.partial(finish, 3),
        tile,
        (section, columns, offset_gain, *state, third),
        scalars=1,
    )
    return out[None]


def solution(mesh):
    in_specs = (P("sec", "tile", None), P("sec", "tile"), P("sec"), P())
    out_specs = P("sec", "tile", None)

    def step(*arrays):
        return shards(*arrays)

    step = jax.shard_map(step, mesh=mesh, in_specs=in_specs, out_specs=out_specs, check_vma=False)
    return step
```

```python
import functools
import math

import jax
import jax.numpy as jnp
from jax import lax
from jax.experimental import pallas as pl
from jax.experimental.pallas import tpu as pltpu
from jax.sharding import PartitionSpec as P


score_factor = 2.5
unusable = 32.0
usable_limit = 16.0
lanes = 128
sublanes = 8
row_block = 256
vmem = pl.BlockSpec(memory_space=pltpu.VMEM)
smem = pl.BlockSpec(memory_space=pltpu.SMEM)
grant = pltpu.CompilerParams(vmem_limit_bytes=24 * 2**20)


def from_behind(block, distance):
    n = lax.axis_size("sec")
    return lax.ppermute(block, "sec", [((i - distance) % n, i) for i in range(n)])


def over_both(block, route):
    n, tiles = lax.axis_size("sec"), lax.axis_size("tile")
    pairs = []
    for i in range(n):
        for t in range(tiles):
            to_section, to_tile = route(i, t, n)
            pairs.append((i * tiles + t, to_section * tiles + to_tile))
    return lax.ppermute(block, ("sec", "tile"), pairs)


def up_and_down(block, parity):
    def route(i, t, n):
        to = i + 2 if t % 2 == parity else i - 2
        return (to, t) if 0 <= to < n else (i, t ^ 1)

    return over_both(block, route)


def swapped(block, first):
    def route(i, t, n):
        to = i + 1 if i % 2 == first else i - 1
        return (to, t) if 0 <= to < n else (i, t ^ 1)

    return over_both(block, route)


def from_partner(block, distance):
    n = lax.axis_size("tile")
    return lax.ppermute(block, "tile", [(i ^ distance, i) for i in range(n)])


def widen(column, channels):
    return jnp.concatenate([column] * (channels // lanes), axis=1)


def is_usable(tile_ref):
    mark = tile_ref[0:8, 0:lanes].astype(jnp.float32)[0:1, :]
    return jnp.where(mark <= usable_limit, 1.0, 0.0)


def matched(query_rows, key_refs, scale, num_rows):
    step = scale * math.log2(math.e)
    blocks = [slice(row, row + row_block) for row in range(0, num_rows, row_block)]

    def scored(rows):
        queries = query_rows(rows)
        return [
            lax.dot_general(
                queries, k[...], (((1,), (1,)), ((), ())), preferred_element_type=jnp.float32
            )
            for k in key_refs
        ]

    scores = scored(blocks[0])
    for rows, rows_after in zip(blocks, blocks[1:] + [None]):
        scores_after = None if rows_after is None else scored(rows_after)
        top = functools.reduce(jnp.maximum, [s.max(axis=1, keepdims=True) for s in scores]) * step
        total = 0.0
        weighted = 0.0
        for s, k in zip(scores, key_refs):
            weights = jnp.exp2(s * step - top)
            total = total + jnp.sum(weights, axis=1, keepdims=True)
            weighted = weighted + jnp.dot(
                weights.astype(jnp.bfloat16), k[...], preferred_element_type=jnp.float32
            )
        yield rows, weighted, total
        scores = scores_after


def chosen_rows(columns, offset, section_ref, usable):
    behind = (section_ref[0] >= offset).astype(jnp.float32)
    bits = (columns >> (offset - 1)) & 1
    return bits.astype(jnp.float32) * (usable * behind)


def note(validity_ref, mark_ref):
    mark_ref[...] = jnp.broadcast_to(validity_ref[...].astype(jnp.float32), mark_ref.shape)


def prepare(select_ref, columns_ref):
    rows = jnp.broadcast_to(select_ref[...].astype(jnp.float32), (lanes, select_ref.shape[1]))
    columns_ref[...] = rows.T.astype(jnp.int32)


def answer(scale, num_sections, section_ref, flag_ref, beside_ref, across_ref, *refs):
    *key_refs, out_ref = refs
    num_rows, channels = out_ref.shape
    section = section_ref[0]
    needed = (section >= 2) & (section < num_sections - 1)

    @pl.when(needed)
    def _():
        keep = jnp.broadcast_to(widen(flag_ref[0:1, :], channels), (row_block, channels)) > 0.5

        def queries(rows):
            return jnp.where(section % 2 == 1, across_ref[rows, :], beside_ref[rows, :])

        for rows, weighted, total in matched(queries, key_refs, scale, num_rows):
            out_ref[rows, :] = jnp.where(keep, weighted / total, unusable).astype(jnp.bfloat16)

    @pl.when(jnp.logical_not(needed))
    def _():
        out_ref[...] = jnp.full(out_ref.shape, unusable, jnp.bfloat16)


def fold(offset, first, scale, section_ref, flag_ref, query_ref, columns_ref, gain_ref, *refs):
    if not first:
        numerator_ref, count_ref, *refs = refs
    *key_refs, out_ref, count_out_ref = refs
    num_rows, channels = query_ref.shape
    usable = flag_ref[0:1, :]
    gain = gain_ref[offset - 1 : offset, :]
    needed = section_ref[0] >= offset

    @pl.when(needed)
    def _():
        for rows, weighted, total in matched(lambda r: query_ref[r, :], key_refs, scale, num_rows):
            count = chosen_rows(columns_ref[rows, :], offset, section_ref, usable)
            numerator = weighted * widen(count / total, channels) * gain
            if not first:
                numerator = numerator + numerator_ref[rows, :]
                count = count + count_ref[rows, :]
            out_ref[rows, :] = numerator
            count_out_ref[rows, :] = count

    @pl.when(jnp.logical_not(needed))
    def _():
        if first:
            out_ref[...] = jnp.zeros_like(out_ref)
            count_out_ref[...] = jnp.zeros_like(count_out_ref)
        else:
            out_ref[...] = numerator_ref[...]
            count_out_ref[...] = count_ref[...]


def finish(
    offset,
    section_ref,
    columns_ref,
    gain_ref,
    numerator_ref,
    count_ref,
    warped_ref,
    out_ref,
    block_ref,
    sems,
):
    num_rows, channels = warped_ref.shape
    usable = is_usable(warped_ref)
    gain = gain_ref[offset - 1 : offset, :]
    copies = []
    for at, row in enumerate(range(0, num_rows, row_block)):
        rows = slice(row, row + row_block)
        chosen = chosen_rows(columns_ref[rows, :], offset, section_ref, usable)
        divisor = jnp.maximum(count_ref[rows, :] + chosen, 1.0)
        numerator = numerator_ref[rows, :] + (
            warped_ref[rows, :].astype(jnp.float32) * widen(chosen, channels) * gain
        )
        block_ref[rows, :] = (numerator / widen(divisor, channels)).astype(jnp.bfloat16)
        part = pl.ds(row, row_block)
        copies.append(
            pltpu.make_async_copy(block_ref.at[part, :], out_ref.at[part, :], sems.at[at])
        )
        copies[-1].start()
    for copy in copies:
        copy.wait()


def shards(features, select, validity, offset_gain):
    queries = features[0]
    num_rows, channels = queries.shape
    scale = score_factor / math.sqrt(channels)
    section = lax.axis_index("sec").astype(jnp.int32)[None]
    wide = jax.ShapeDtypeStruct((num_rows, channels), jnp.float32)
    tile = jax.ShapeDtypeStruct((num_rows, channels), jnp.bfloat16)
    narrow = jax.ShapeDtypeStruct((num_rows, lanes), jnp.float32)
    keys = num_rows * lax.axis_size("tile")
    heavy = pl.CostEstimate(
        flops=4 * num_rows * keys * channels,
        transcendentals=num_rows * keys,
        bytes_accessed=2 * keys * channels,
    )

    def call(body, out, args, cost=None, scalars=0):
        return pl.pallas_call(
            body,
            out_shape=out,
            in_specs=[smem] * scalars + [vmem] * (len(args) - scalars),
            out_specs=jax.tree.map(lambda _: vmem, out),
            cost_estimate=cost,
            compiler_params=grant,
        )(*args)

    def all_tiles(t):
        tiles = [t]
        distance = lax.axis_size("tile") // 2
        while distance:
            for held in tuple(tiles):
                tiles.append(from_partner(held, distance))
            distance //= 2
        return tiles

    columns_shape = jax.ShapeDtypeStruct((num_rows, lanes), jnp.int32)
    mark_shape = jax.ShapeDtypeStruct((sublanes, lanes), jnp.float32)
    columns = call(prepare, columns_shape, (select,))
    mark = call(note, mark_shape, (validity[:, None],))
    even_up = up_and_down(queries, 0)
    odd_up = up_and_down(queries, 1)
    second = jnp.where(lax.axis_index("tile") % 2 == 0, even_up, odd_up)
    beside = swapped(queries, 0)
    across = swapped(queries, 1)
    flag1 = from_behind(mark, 1)
    flag2 = from_behind(mark, 2)
    first = jnp.where(section[0] % 2 == 1, beside, across)
    second_tiles = all_tiles(second)
    first_tiles = all_tiles(first)
    answered = call(
        functools.partial(answer, scale, lax.axis_size("sec")),
        tile,
        (section, flag2, beside, across, *second_tiles),
        heavy,
        1,
    )
    n = lax.axis_size("sec")
    routes = [(i, i + 1) for i in range(2, n - 1)] + [(0, 2), (1, 0), (n - 1, 1)]
    third = lax.ppermute(answered, "sec", routes)
    common = (queries, columns, offset_gain)
    state = call(
        functools.partial(fold, 2, True, scale),
        (wide, narrow),
        (section, flag2, *common, *second_tiles),
        heavy,
        1,
    )
    state = call(
        functools.partial(fold, 1, False, scale),
        (wide, narrow),
        (section, flag1, *common, *state, *first_tiles),
        heavy,
        1,
    )
    args = (section, columns, offset_gain, *state, third)
    out = pl.pallas_call(
        functools.partial(finish, 3),
        out_shape=tile,
        in_specs=[smem] + [vmem] * (len(args) - 1),
        out_specs=pl.BlockSpec(memory_space=pl.ANY),
        scratch_shapes=[
            pltpu.VMEM((num_rows, channels), jnp.bfloat16),
            pltpu.SemaphoreType.DMA((num_rows // row_block,)),
        ],
        compiler_params=grant,
        name="finish",
    )(*args)
    return out[None]


def solution(mesh):
    in_specs = (P("sec", "tile", None), P("sec", "tile"), P("sec"), P())
    out_specs = P("sec", "tile", None)

    def step(*arrays):
        return shards(*arrays)

    step = jax.shard_map(step, mesh=mesh, in_specs=in_specs, out_specs=out_specs, check_vma=False)
    return step
```
